512 devices in a mesh: tower: 8 (over z_hi, core), group: 4 (over x), blk: 16 (over y, z_lo).
Axes of the slice: x: 4, y: 8, z: 8 (z_hi: 4, z_lo: 2; z = z_hi * 2 + z_lo), core: 2. Of those that a mesh axis runs over, the one named last changes fastest.
Arguments:
- queries: bfloat16 [2048, 384, 256], P(('tower', 'group', 'blk')), may hold values from -102 to 102
- cluster_ids: int32 [2048, 64], P(('tower', 'group', 'blk')), may hold values from 0 to 127, all different within a row
- positives: int32 [2048, 384], P(('tower', 'group', 'blk')), may hold values from 0 to 1023
- owner_map: int32 [4, 128], P('group'), may hold values from 0 to 127, each once within a row
- panels: bfloat16 [512, 16, 256], P(('group', 'blk')), may hold values from -0.375 to 0.375
- scales: bfloat16 [512, 16], P(('group', 'blk')), may hold values from 0.5 to 2
Outputs:
- losses: bfloat16 [2048, 384], P(('tower', 'group', 'blk'))
- query_grads: bfloat16 [2048, 384, 256], P(('tower', 'group', 'blk'))
- panel_grads: float32 [512, 16, 256], P(('group', 'blk'), 'tower')
The draws below stay inside these ranges and needn't reach their ends.
Inputs may be any that keep to these rules, and one draw needn't show every extreme that they name: `cluster_ids`: each row lists 64 different clusters. `owner_map`: each row is a permutation.
All inputs are finite; a program needn't handle non-finite values.
Results may differ from the reference program's by a relative error of at most 0.014.
Values may be sent and summed in bfloat16 or wider, within the bound.
A program may use at most 64 MiB of HBM per device.

```python
import math
import jax
import jax.numpy as jnp
from jax import lax

D = 256
ITEMS = 16
NSEL = 64
CLG = 128
QB = 384
BPG = 1
NQB = 2048
NCL = 512
N_GROUP = 4


def draw_queries(key, part):
    subkeys = jax.random.split(key, 1)
    shape = (NQB, QB, D)
    values = jnp.clip(jax.random.normal(subkeys[0], shape, jnp.float32), -6.0, 6.0)
    return values.astype(jnp.bfloat16)


def set_ends(values, stream_key, low, largest):
    longest = values.shape.index(max(values.shape))
    spots = []
    for shift in (0, 1):
        where = [jax.random.randint(jax.random.fold_in(stream_key, axis), (), 0, length) for axis, length in enumerate(values.shape)]
        where[longest] = (where[longest] + shift) % values.shape[longest]
        spots.append(tuple(where))
    return values.at[spots[0]].set(low).at[spots[1]].set(largest)


def steps_of(key, dims, pieces, least, largest):
    factor_of = 1.0
    for dim, shards_of in pieces:
        heights = jax.random.uniform(jax.random.fold_in(jax.random.fold_in(key, 6), dim), (shards_of,), jnp.float32, least / len(pieces), largest / len(pieces))
        factor_of = factor_of * jnp.repeat(jnp.exp(heights), dims[dim] // shards_of).reshape((-1,) + (1,) * (len(dims) - 1 - dim))
    return factor_of


def choose_distinct(rng, rows, count, top, lift):
    ranking = jax.random.permutation(jax.random.fold_in(rng, 1), count)
    boost = ranking
    for power in range(3):
        boost = boost * boost // count
    boost = boost * lift // count
    lots = jax.random.randint(jax.random.fold_in(rng, 2), (rows, count), 0, 4096) + boost
    sure = jax.random.permutation(jax.random.fold_in(rng, 3), rows)[jnp.arange(count) % rows]
    lots = jnp.where(jnp.arange(rows)[:, None] == sure[None, :], 1 << 14, lots)
    score = lots * count + jnp.arange(count)
    return lax.top_k(score.astype(jnp.int32), top)[1].astype(jnp.int32)


def normal_values(rng, extent, width, most, cuts=(), held_as=jnp.bfloat16):
    array = jax.random.normal(rng, extent, jnp.float32) * width
    if len(cuts) > 0:
        array = steps_of(rng, extent, cuts, -0.22, 0.18) * array
    return jnp.clip(array, min=-most, max=most).astype(held_as)


def setup_inputs(seed: int = 0) -> dict:
    keys = jax.random.split(jax.random.key(seed), 7)
    return {
        "queries": draw_queries(jax.random.fold_in(keys[6], 71), 0),
        "cluster_ids": choose_distinct(keys[1], NQB, CLG, NSEL, 8192),
        "positives": set_ends(jax.random.randint(keys[2], (NQB, QB), 0, NSEL * ITEMS), jax.random.fold_in(keys[2], 1), 0, (NSEL * ITEMS) - 1).astype(jnp.int32),
        "owner_map": jax.vmap(lambda own: jax.random.permutation(own, CLG))(jax.random.split(keys[3], N_GROUP)).reshape((N_GROUP, CLG)).astype(jnp.int32),
        "panels": normal_values(keys[4], (NCL, ITEMS, D), D ** -0.5, 0.375, ((0, 64),)),
        "scales": jnp.clip(jnp.exp(math.log(2.0) - 1.3862944 * jax.random.uniform(keys[5], (NCL, ITEMS), jnp.float32) ** steps_of(keys[5], (NCL, ITEMS), ((0, 64),), -0.2, 0.2)), 0.5, 2.0).astype(jnp.bfloat16),
    }


def reference(queries, cluster_ids, positives, owner_map, panels, scales):
    block_dev = BPG * N_GROUP

    def one_block(panel_grads, inputs):
        block_query, block_ids, block_pos, block_index = inputs
        group_index = (block_index % block_dev) // BPG
        panel_slots = owner_map[group_index][block_ids]
        clusters = (group_index * CLG + panel_slots).astype(jnp.int32)
        candidates = panels[clusters].reshape(NSEL * ITEMS, D)
        cand_scale = scales[clusters].reshape(NSEL * ITEMS).astype(jnp.float32)
        scores = jnp.dot(block_query, candidates.T, preferred_element_type=jnp.float32) * cand_scale[None, :]
        row_peak = jnp.max(scores, axis=1, keepdims=True)
        log_total = row_peak[:, 0] + jnp.log(jnp.sum(jnp.exp(scores - row_peak), axis=1))
        picked = jnp.take_along_axis(scores, block_pos[:, None], axis=1)[:, 0]
        losses = (log_total - picked).astype(jnp.bfloat16)
        onehot = (jnp.arange(NSEL * ITEMS, dtype=jnp.int32)[None, :] == block_pos[:, None]).astype(jnp.float32)
        weights = ((jnp.exp(scores - log_total[:, None]) - onehot) * cand_scale[None, :]).astype(jnp.bfloat16)
        query_grad = jnp.dot(weights, candidates, preferred_element_type=jnp.float32).astype(jnp.bfloat16)
        grad_term = jnp.dot(weights.T, block_query, preferred_element_type=jnp.float32).reshape(NSEL, ITEMS, D)
        panel_grads = panel_grads.at[clusters].add(grad_term)
        return panel_grads, (losses, query_grad)

    zero_grads = jnp.zeros((NCL, ITEMS, D), jnp.float32)
    indices = jnp.arange(NQB, dtype=jnp.int32)
    panel_grads, (losses, query_grads) = lax.scan(one_block, zero_grads, (queries, cluster_ids, positives, indices))
    return losses, query_grads, panel_grads
```

```python
import functools

import jax
import jax.numpy as jnp
from jax import lax
from jax.experimental import pallas as pl
from jax.experimental.pallas import tpu as pltpu
from jax.sharding import PartitionSpec as P

MESH = pl.DeviceIdType.MESH
NX, NY, NZ = 4, 8, 8


def place():
    t, g, b = lax.axis_index("tower"), lax.axis_index("group"), lax.axis_index("blk")
    core, y = lax.rem(t, 2), lax.div(b, 2)
    z = 2 * lax.div(t, 2) + lax.rem(b, 2)
    return t, g, b, core, y, z


def at_yz(core, g, y, z):
    return (2 * lax.div(z, 2) + core, g, 2 * y + lax.rem(z, 2))


def barrier_with(peers):
    sem = pltpu.get_barrier_semaphore()
    for peer in peers:
        pl.semaphore_signal(sem, inc=1, device_id=peer, device_id_type=MESH)
    pl.semaphore_wait(sem, len(peers))


def remote(src, dst, send, recv, peer):
    return pltpu.make_async_remote_copy(
        src_ref=src, dst_ref=dst, send_sem=send, recv_sem=recv, device_id=peer, device_id_type=MESH
    )


def exchange_kernel(
    q, ids, pos, pan, sc,
    qo, ido, poso, pano, sco,
    loc, xs, xr, ys, yr, yss, yrs, zs, zr, zss, zrs, ps, pr,
):
    t, g, b, core, y, z = place()
    partner = (t + 1 - 2 * core, g, b)
    zl = lax.rem(z, 2)
    step = 1 - 2 * core
    z_to = at_yz(core, g, y, lax.rem(z + step + NZ, NZ))
    z_from = at_yz(core, g, y, lax.rem(z - step + NZ, NZ))
    x_peers = [(t, lax.rem(g + d, NX), b) for d in range(1, NX)]
    y_peers = [at_yz(core, g, lax.rem(y + d, NY), z) for d in range(1, NY)]
    local = [
        pltpu.make_async_copy(pan, pano.at[b], loc.at[0]),
        pltpu.make_async_copy(sc, sco.at[b], loc.at[1]),
        pltpu.make_async_copy(q.at[g], qo.at[g], loc.at[2]),
        pltpu.make_async_copy(ids.at[g], ido.at[g], loc.at[3]),
        pltpu.make_async_copy(pos.at[g], poso.at[g], loc.at[4]),
    ]
    for copy in local:
        copy.start()
    barrier_with(x_peers + y_peers + [z_to, z_from, partner])

    half = pl.ds(core * 4, 4)
    mine = pano.at[b, half]
    y_copies, z_copies, p_copies = [], [], []
    z_copies.append(remote(pan.at[half], mine, zs.at[0], zr.at[0], z_to))
    z_copies[0].start()
    z_scale = [remote(sc, sco.at[b], zss.at[0], zrs.at[0], z_to)]
    z_scale[0].start()
    y_scale = []
    for d in (4, 3, 5, 2, 6, 1, 7):
        y_copies.append((d, remote(pan.at[half], mine, ys.at[d - 1], yr.at[d - 1], y_peers[d - 1])))
        y_copies[-1][1].start()
        y_scale.append((d, remote(sc, sco.at[b], yss.at[d - 1], yrs.at[d - 1], y_peers[d - 1])))
        y_scale[-1][1].start()
    x_copies = []
    for d in (2, 1, 3):
        peer, dst = x_peers[d - 1], lax.rem(g + d, NX)
        for n, (src, out) in enumerate(((pos, poso), (ids, ido), (q, qo))):
            x_copies.append(remote(src.at[dst], out.at[g], xs.at[d - 1, n], xr.at[d - 1, n], peer))
            x_copies[-1].start()

    order = (1, 7, 2, 6, 3, 5, 4)
    by_d = dict(y_copies)
    scale_by_d = dict(y_scale)
    for n, d in enumerate(order):
        src = 2 * lax.rem(y - d + NY, NY) + zl
        piece = pano.at[src, half]
        by_d[d].wait_recv()
        z_copies.append(remote(piece, piece, zs.at[n + 1], zr.at[n + 1], z_to))
        z_copies[-1].start()
        p_copies.append(remote(piece, piece, ps.at[n], pr.at[n], partner))
        p_copies[-1].start()
        scale_by_d[d].wait_recv()
        z_scale.append(remote(sco.at[src], sco.at[src], zss.at[n + 1], zrs.at[n + 1], z_to))
        z_scale[-1].start()
    for n, d in enumerate((0,) + order):
        src = 2 * lax.rem(y - d + NY, NY) + 1 - zl
        piece = pano.at[src, half]
        z_copies[n].wait_recv()
        p_copies.append(remote(piece, piece, ps.at[7 + n], pr.at[7 + n], partner))
        p_copies[-1].start()
        z_scale[n].wait_recv()
    for copy in p_copies + x_copies:
        copy.wait_recv()
    for copy in local:
        copy.wait()
    for copy in [c for _, c in y_copies + y_scale] + z_copies + z_scale + p_copies + x_copies:
        copy.wait_send()


def compute_kernel(
    ids, owner, q_ref, pos_ref, pan_ref, sc_ref, qg_ref, loss_ref, grs_ref, tab, cand, sbuf, wbuf, acc
):
    items, sel = 16, ids.shape[2]
    rows = q_ref.shape[1]
    sub = lax.broadcasted_iota(jnp.int32, (items, rows), 0)
    eye = (
        lax.broadcasted_iota(jnp.int32, (items, items), 0)
        == lax.broadcasted_iota(jnp.int32, (items, items), 1)
    ).astype(jnp.float32)
    for n in range(sc_ref.shape[0]):
        part = sc_ref[n].astype(jnp.float32)
        column = jnp.sum(part[:, None, :] * eye[None], axis=2, keepdims=True)
        tab[pl.ds(8 * n, 8)] = jnp.broadcast_to(column, (8, items, 128))
    acc[...] = jnp.zeros_like(acc)

    def wide(slot):
        one = tab[slot]
        return jnp.concatenate([one] * (rows // 128), axis=1)

    def block(n, carry):
        slots = [owner[0, ids[n, 0, j]] for j in range(sel)]
        for j in range(sel):
            cand[pl.ds(items * j, items), :] = pan_ref[slots[j]]
        q = q_ref[n]
        sbuf[...] = lax.dot_general(
            cand[...], q, (((1,), (1,)), ((), ())), preferred_element_type=jnp.float32
        )
        peak = jnp.full((items, rows), -jnp.inf, jnp.float32)
        for j in range(sel):
            at = pl.ds(items * j, items)
            s = sbuf[at, :] * wide(slots[j])
            sbuf[at, :] = s
            peak = jnp.maximum(peak, s)
        peak = jnp.max(peak, axis=0, keepdims=True)
        pos = pos_ref[n]
        rel = jnp.broadcast_to(pos, (items, rows)) - sub
        total = jnp.zeros((items, rows), jnp.float32)
        picked = jnp.zeros((items, rows), jnp.float32)
        for j in range(sel):
            at = pl.ds(items * j, items)
            s = sbuf[at, :]
            picked = jnp.where(rel == items * j, s, picked)
            e = jnp.exp(s - peak)
            sbuf[at, :] = e
            total = total + e
        total = jnp.sum(total, axis=0, keepdims=True)
        picked = jnp.sum(picked, axis=0, keepdims=True)
        loss_ref[n] = peak + jnp.log(total) - picked
        inverse = 1.0 / total
        for j in range(sel):
            at = pl.ds(items * j, items)
            chance = sbuf[at, :] * inverse
            w = jnp.where(rel == items * j, chance - 1.0, chance) * wide(slots[j])
            wbuf[at, :] = w.astype(jnp.bfloat16)
        w = wbuf[...]
        grad = jnp.dot(w, q, preferred_element_type=jnp.float32)
        for j in range(sel):
            acc[slots[j]] += grad[items * j : items * (j + 1)]
        qg_ref[n] = lax.dot_general(
            w, cand[...], (((0,), (0,)), ((), ())), preferred_element_type=jnp.float32
        ).astype(jnp.bfloat16)
        return carry

    lax.fori_loop(0, q_ref.shape[0], block, 0)

    low = lax.broadcasted_iota(jnp.int32, (8, 256), 0) < 4

    def pack(y, carry):
        for zl in range(2):
            for h in range(2):
                base = (2 * y + zl) * 8 + 4 * h
                for v in range(2):
                    tiles = ([], [])
                    for sp in range(2):
                        a = acc[base + 2 * sp, 8 * v : 8 * v + 8, :]
                        c = acc[base + 2 * sp + 1, 8 * v : 8 * v + 8, :]
                        tiles[0].append(jnp.where(low, a, pltpu.roll(c, 4, axis=0)))
                        tiles[1].append(jnp.where(low, pltpu.roll(a, 4, axis=0), c))
                    for k in range(2):
                        z = 2 * (2 * v + k) + zl
                        tile = jnp.concatenate(tiles[k], axis=0).astype(jnp.bfloat16)
                        grs_ref[h, 0, y, z] = tile[:, :128]
                        grs_ref[h, 1, z, y] = tile[:, 128:]
        return carry

    lax.fori_loop(0, NY, pack, 0)


def reduce_kernel(
    grs, qg, loss_in, loss_out, qg_out, pg_out,
    r0, s0, r1, s1, r2, fin, rfin, lbuf,
    loc, cs, cr, fs, fr, s1s, s1r, s2s, s2r, xs, xr,
):
    t, g, b, core, y, z = place()
    partner = (t + 1 - 2 * core, g, b)
    x_peers = [(t, lax.rem(g + d, NX), b) for d in range(1, NX)]
    y_peers = [at_yz(core, g, lax.rem(y + d, NY), z) for d in range(1, NY)]
    z_peers = [at_yz(core, g, y, lax.rem(z + d, NZ)) for d in range(1, NZ)]
    local = [
        pltpu.make_async_copy(qg.at[g], qg_out.at[g], loc.at[0]),
        pltpu.make_async_copy(loss_in.at[g], lbuf.at[g], loc.at[1]),
    ]
    for copy in local:
        copy.start()
    barrier_with(x_peers + y_peers + z_peers + [partner])
    firsts = []
    for f in range(2):
        firsts.append(remote(grs.at[1 - core, f], r0.at[f], cs.at[f], cr.at[f], partner))
        firsts[f].start()
    backs = []
    for d in (2, 1, 3):
        peer, dst = x_peers[d - 1], lax.rem(g + d, NX)
        for n, (src, out) in enumerate(((loss_in, lbuf), (qg, qg_out))):
            backs.append(remote(src.at[dst], out.at[g], xs.at[d - 1, n], xr.at[d - 1, n], peer))
            backs[-1].start()
    here = (y, z)
    ahead = (y_peers, z_peers)
    stage1 = []
    for f in range(2):
        firsts[f].wait_recv()
        for k in range(NY):
            s0[f, k] = (
                grs[core, f, k].astype(jnp.float32) + r0[f, k].astype(jnp.float32)
            ).astype(jnp.bfloat16)
        for d in (4, 3, 5, 2, 6, 1, 7):
            copy = remote(
                s0.at[f, lax.rem(here[f] + d, 8)], r1.at[f, d - 1],
                s1s.at[f, d - 1], s1r.at[f, d - 1], ahead[f][d - 1],
            )
            copy.start()
            stage1.append(copy)
    stage2 = []
    for f in range(2):
        total = s0[f, here[f]].astype(jnp.float32)
        for copy in stage1[7 * f : 7 * f + 7]:
            copy.wait_recv()
        for d in range(7):
            total = total + r1[f, d].astype(jnp.float32)
        s1[f] = total.astype(jnp.bfloat16)
        for d in (4, 3, 5, 2, 6, 1, 7):
            copy = remote(
                s1.at[f, lax.rem(here[1 - f] + d, 8)], r2.at[f, d - 1],
                s2s.at[f, d - 1], s2r.at[f, d - 1], ahead[1 - f][d - 1],
            )
            copy.start()
            stage2.append(copy)
    for f in range(2):
        total = s1[f, here[1 - f]].astype(jnp.float32)
        for copy in stage2[7 * f : 7 * f + 7]:
            copy.wait_recv()
        for d in range(7):
            total = total + r2[f, d].astype(jnp.float32)
        fin[f] = total
    last = remote(fin, rfin, fs, fr, partner)
    last.start()
    for copy in local:
        copy.wait()
    for copy in backs:
        copy.wait_recv()
    for n in range(NX):
        loss_out[n : n + 1, :] = lbuf[n].astype(jnp.bfloat16)
    last.wait_recv()
    for h in range(2):
        for f in range(2):
            tile = jnp.where(core == h, fin[f], rfin[f])
            for k in range(4):
                rows = jnp.where(core == 0, tile[4 * k : 4 * k + 2], tile[4 * k + 2 : 4 * k + 4])
                pg_out[4 * h + k, :, 128 * f : 128 * f + 128] = rows
    for copy in firsts + stage1 + stage2 + backs + [last]:
        copy.wait_send()


def shards(queries, cluster_ids, positives, owner_map, panels, scales):
    count, rows, width = queries.shape
    slots, items = scales.shape
    blks = lax.axis_size("blk")
    sel = cluster_ids.shape[1]
    dma = pltpu.SemaphoreType.DMA
    anyspec = pl.BlockSpec(memory_space=pl.ANY)
    vmem = pl.BlockSpec(memory_space=pltpu.VMEM)
    smem = pl.BlockSpec(memory_space=pltpu.SMEM)
    f32, bf16, i32 = jnp.float32, jnp.bfloat16, jnp.int32
    sds = jax.ShapeDtypeStruct

    q_all, ids_all, pos_all, pan_all, sc_all = pl.pallas_call(
        exchange_kernel,
        out_shape=(
            sds((count, rows, width), bf16),
            sds((count, 1, sel), i32),
            sds((count, 1, rows), i32),
            sds((blks, slots, items, width), bf16),
            sds((blks, slots, items), bf16),
        ),
        in_specs=[anyspec] * 5,
        out_specs=(vmem,) * 5,
        scratch_shapes=[
            dma((5,)), dma((3, 3)), dma((3, 3)), dma((7,)), dma((7,)), dma((7,)), dma((7,)),
            dma((8,)), dma((8,)), dma((8,)), dma((8,)), dma((15,)), dma((15,)),
        ],
        compiler_params=pltpu.CompilerParams(
            collective_id=0, has_side_effects=True, vmem_limit_bytes=8 << 20
        ),
        name="exchange",
    )(queries, cluster_ids.reshape(count, 1, sel), positives.reshape(count, 1, rows), panels, scales)

    qg, loss, grs = pl.pallas_call(
        compute_kernel,
        out_shape=(
            sds((count, rows, width), bf16),
            sds((count, 1, rows), f32),
            sds((2, 2, 8, 8, 16, 128), bf16),
        ),
        in_specs=[smem, smem, vmem, vmem, vmem, vmem],
        out_specs=(vmem,) * 3,
        scratch_shapes=[
            pltpu.VMEM((blks * slots, items, 128), f32),
            pltpu.VMEM((sel * items, width), bf16),
            pltpu.VMEM((sel * items, rows), f32),
            pltpu.VMEM((sel * items, rows), bf16),
            pltpu.VMEM((blks * slots, items, width), f32),
        ],
        compiler_params=pltpu.CompilerParams(vmem_limit_bytes=24 << 20),
        name="score",
    )(ids_all, owner_map, q_all, pos_all, pan_all.reshape(blks * slots, items, width), sc_all)

    return pl.pallas_call(
        reduce_kernel,
        out_shape=(
            sds((count, rows), bf16),
            sds((count, rows, width), bf16),
            sds((slots, 2, width), f32),
        ),
        in_specs=[vmem, vmem, vmem],
        out_specs=(vmem, anyspec, vmem),
        scratch_shapes=[
            pltpu.VMEM((2, 8, 8, 16, 128), bf16),
            pltpu.VMEM((2, 8, 8, 16, 128), bf16),
            pltpu.VMEM((2, 7, 8, 16, 128), bf16),
            pltpu.VMEM((2, 8, 16, 128), bf16),
            pltpu.VMEM((2, 7, 16, 128), bf16),
            pltpu.VMEM((2, 16, 128), f32),
            pltpu.VMEM((2, 16, 128), f32),
            pltpu.VMEM((count, 1, rows), f32),
            dma((2,)), dma((2,)), dma((2,)), dma, dma, dma((2, 7)), dma((2, 7)), dma((2, 7)), dma((2, 7)),
            dma((3, 2)), dma((3, 2)),
        ],
        compiler_params=pltpu.CompilerParams(
            collective_id=1, has_side_effects=True, vmem_limit_bytes=16 << 20
        ),
        name="reduce",
    )(grs, qg, loss)


def solution(mesh):
    return jax.shard_map(
        shards,
        mesh=mesh,
        in_specs=(
            P(("tower", "group", "blk"), None, None),
            P(("tower", "group", "blk"), None),
            P(("tower", "group", "blk"), None),
            P("group", None),
            P(("group", "blk"), None, None),
            P(("group", "blk"), None),
        ),
        out_specs=(
            P(("tower", "group", "blk"), None),
            P(("tower", "group", "blk"), None, None),
            P(("group", "blk"), "tower", None),
        ),
        check_vma=False,
    )
```

```python
import jax
import jax.numpy as jnp
from jax import lax
from jax.experimental import pallas as pl
from jax.experimental.pallas import tpu as pltpu
from jax.sharding import PartitionSpec as P

MESH = pl.DeviceIdType.MESH
NX, NY, NZ = 4, 8, 8
FAR_FIRST = (4, 3, 5, 2, 6, 1, 7)


def remote(src, dst, send, recv, peer):
    return pltpu.make_async_remote_copy(
        src_ref=src, dst_ref=dst, send_sem=send, recv_sem=recv, device_id=peer, device_id_type=MESH
    )


def signal(sem, peer):
    pl.semaphore_signal(sem, inc=1, device_id=peer, device_id_type=MESH)


def score_block(n, row, slots, q_ref, pos_ref, pan_ref, tab, cand, sbuf, wbuf, gbuf, loss_ref):
    items, sel, rows = 16, len(slots), q_ref.shape[1]
    sub = lax.broadcasted_iota(jnp.int32, (items, rows), 0)

    def wide(slot):
        one = tab[slot]
        return jnp.concatenate([one] * (rows // 128), axis=1)

    for j in range(sel):
        cand[n, pl.ds(items * j, items), :] = pan_ref[slots[j]]
    q = q_ref[n]
    sbuf[...] = lax.dot_general(
        cand[n], q, (((1,), (1,)), ((), ())), preferred_element_type=jnp.float32
    )
    peak = jnp.full((items, rows), -jnp.inf, jnp.float32)
    for j in range(sel):
        at = pl.ds(items * j, items)
        s = sbuf[at, :] * wide(slots[j])
        sbuf[at, :] = s
        peak = jnp.maximum(peak, s)
    peak = jnp.max(peak, axis=0, keepdims=True)
    pos = pos_ref[n, pl.ds(row, 1), :]
    rel = jnp.broadcast_to(pos, (items, rows)) - sub
    total = jnp.zeros((items, rows), jnp.float32)
    picked = jnp.zeros((items, rows), jnp.float32)
    for j in range(sel):
        at = pl.ds(items * j, items)
        s = sbuf[at, :]
        picked = jnp.where(rel == items * j, s, picked)
        e = jnp.exp(s - peak)
        sbuf[at, :] = e
        total = total + e
    total = jnp.sum(total, axis=0, keepdims=True)
    picked = jnp.sum(picked, axis=0, keepdims=True)
    loss_ref[n] = peak + jnp.log(total) - picked
    inverse = 1.0 / total
    for j in range(sel):
        at = pl.ds(items * j, items)
        chance = sbuf[at, :] * inverse
        w = jnp.where(rel == items * j, chance - 1.0, chance) * wide(slots[j])
        wbuf[n, at, :] = w.astype(jnp.bfloat16)
    grad = jnp.dot(wbuf[n], q, preferred_element_type=jnp.float32)
    gbuf[n, pl.ds(0, sel)] = grad.reshape(sel, items, grad.shape[1])


def main_kernel(
    owner, q, ids, pos, pan, sc,
    qg_out, loss_out, fin_out, rfin,
    qo, ido, poso, pano, sco, ids_s, tab, cand, sbuf, wbuf, gbuf, lossb, qgb, inv_v, inv_s,
    p0, own0, r0, s0, r1, s1, r2, fin,
    loc, xs, xr, ys, yr, yss, yrs, zs, zr, zss, zrs, ps, pr, ready1, ready2,
    cs, cr, s1s, s1r, s2s, s2r, bs, br, fs, fr,
):
    t, g, b = lax.axis_index("tower"), lax.axis_index("group"), lax.axis_index("blk")
    core, y, zl = lax.rem(t, 2), lax.div(b, 2), lax.rem(b, 2)
    z = 2 * lax.div(t, 2) + zl
    step = 1 - 2 * core

    def at_yz(yy, zz):
        yy, zz = lax.rem(yy + NY, NY), lax.rem(zz + NZ, NZ)
        return (2 * lax.div(zz, 2) + core, g, 2 * yy + lax.rem(zz, 2))

    partner = (t + step, g, b)
    x_peers = [(t, lax.rem(g + d, NX), b) for d in range(1, NX)]
    z_to, z_from = at_yz(y, z + step), at_yz(y, z - step)

    local = [
        pltpu.make_async_copy(pan, pano.at[b], loc.at[0]),
        pltpu.make_async_copy(sc, sco.at[b], loc.at[1]),
        pltpu.make_async_copy(q.at[g], qo.at[g], loc.at[2]),
        pltpu.make_async_copy(ids.at[g], ido.at[g], loc.at[3]),
        pltpu.make_async_copy(pos, poso.at[g], loc.at[4]),
    ]
    near = [at_yz(y + d, z) for d in (2, -2, 1, -1)] + x_peers + [z_to, z_from, partner]
    barrier = pltpu.get_barrier_semaphore()
    for peer in near:
        signal(barrier, peer)
    for copy in local:
        copy.start()
    pl.semaphore_wait(barrier, len(near))
    for peer in (z_to, z_from):
        signal(ready1, peer)

    half = pl.ds(core * 4, 4)
    sends = []

    def send(src, dst, s, r, peer):
        copy = remote(src, dst, s, r, peer)
        copy.start()
        sends.append(copy)
        return copy

    y_in, z_in, p_in = {}, {}, []

    def y_send(d, src_blk, to_y):
        for own, (buf, s, r) in (
            (pan.at[half], (pano.at[src_blk, half], ys, yr)),
            (sc, (sco.at[src_blk], yss, yrs)),
        ):
            src = own if src_blk is b else buf
            y_in.setdefault(d, []).append(send(src, buf, s.at[d - 1], r.at[d - 1], at_yz(to_y, z)))

    def z_send(d, src_blk):
        for own, (buf, s, r) in (
            (pan.at[half], (pano.at[src_blk, half], zs, zr)),
            (sc, (sco.at[src_blk], zss, zrs)),
        ):
            src = own if src_blk is b else buf
            z_in.setdefault(d, []).append(send(src, buf, s.at[d], r.at[d], z_to))

    def p_send(src_blk):
        k = len(p_in)
        piece = pano.at[src_blk, half]
        p_in.append(send(piece, piece, ps.at[k], pr.at[k], partner))

    def blk_at(d, side):
        return 2 * lax.rem(y - d + NY, NY) + side

    y_send(2, b, y + 2)
    y_send(6, b, y - 2)
    y_send(1, b, y + 1)
    y_send(7, b, y - 1)
    z_send(0, b)
    x_in = []
    for d in (2, 1, 3):
        dst = lax.rem(g + d, NX)
        for n, (src, out) in enumerate(
            ((ids.at[dst], ido.at[g]), (pos, poso.at[g]), (q.at[dst], qo.at[g]))
        ):
            x_in.append(send(src, out, xs.at[d - 1, n], xr.at[d - 1, n], x_peers[d - 1]))

    def take_y(d):
        for copy in y_in[d]:
            copy.wait_recv()

    def take_z(d):
        for copy in z_in[d]:
            copy.wait_recv()
        p_send(blk_at(d, 1 - zl))

    for d in (1, 7):
        take_y(d)
        z_send(d, blk_at(d, zl))
        p_send(blk_at(d, zl))
    take_y(2)
    y_send(3, blk_at(2, zl), y + 1)
    take_y(6)
    y_send(5, blk_at(6, zl), y - 1)
    y_send(4, 2 * lax.rem(y - 2 * step + NY, NY) + zl, y + 2 * step)
    for d in (2, 6):
        z_send(d, blk_at(d, zl))
        p_send(blk_at(d, zl))
    take_z(0)
    pl.semaphore_wait(ready1, 2)
    for d in (2, -2):
        signal(ready2, at_yz(y, z + d))
    take_z(1)
    take_z(7)
    for d in (3, 5, 4):
        take_y(d)
        z_send(d, blk_at(d, zl))
        p_send(blk_at(d, zl))
    for d in (2, 6, 3, 5, 4):
        take_z(d)
    for copy in local:
        copy.wait()
    for copy in x_in:
        copy.wait_recv()
    to_smem = pltpu.make_async_copy(ido, ids_s, loc.at[5])
    to_smem.start()

    items = 16
    eye = (
        lax.broadcasted_iota(jnp.int32, (items, items), 0)
        == lax.broadcasted_iota(jnp.int32, (items, items), 1)
    ).astype(jnp.float32)
    for n in range(sco.shape[0]):
        part = sco[n].astype(jnp.float32)
        column = jnp.sum(part[:, None, :] * eye[None], axis=2, keepdims=True)
        tab[pl.ds(8 * n, 8)] = jnp.broadcast_to(column, (8, items, 128))
    sel = ids_s.shape[2]
    for n in range(NX):
        gbuf[n, sel] = jnp.zeros(gbuf.shape[2:], jnp.float32)
    for copy in p_in:
        copy.wait_recv()
    to_smem.wait()
    lane = lax.broadcasted_iota(jnp.int32, (1, 128), 1)

    def block(n, carry):
        slots = [owner[0, ids_s[n, 0, j]] for j in range(sel)]
        where = jnp.full((1, 128), sel, jnp.int32)
        for j in range(sel):
            where = jnp.where(lane == slots[j], j, where)
        inv_v[n] = where
        score_block(n, g, slots, qo, poso, panf(pano), tab, cand, sbuf, wbuf, gbuf, lossb)
        return carry

    lax.fori_loop(0, NX, block, 0)
    inv_copy = pltpu.make_async_copy(inv_v, inv_s, loc.at[6])
    inv_copy.start()
    inv_copy.wait()

    low = lax.broadcasted_iota(jnp.int32, (8, 256), 0) < 4

    def pack(h, out, yy):
        for side in range(2):
            base = (2 * yy + side) * 8 + 4 * h
            rows = []
            for k in range(4):
                total = gbuf[0, inv_s[0, 0, base + k]]
                for n in range(1, NX):
                    total = total + gbuf[n, inv_s[n, 0, base + k]]
                rows.append(total)
            for v in range(2):
                tiles = ([], [])
                for sp in range(2):
                    a = rows[2 * sp][8 * v : 8 * v + 8]
                    c = rows[2 * sp + 1][8 * v : 8 * v + 8]
                    tiles[0].append(jnp.where(low, a, pltpu.roll(c, 4, axis=0)))
                    tiles[1].append(jnp.where(low, pltpu.roll(a, 4, axis=0), c))
                for k in range(2):
                    zz = 2 * (2 * v + k) + side
                    tile = jnp.concatenate(tiles[k], axis=0).astype(out.dtype)
                    out[0, yy, zz] = tile[:, :128]
                    out[1, zz, yy] = tile[:, 128:]

    def pack_away(yy, carry):
        pack(1 - core, p0, yy)
        return carry

    def pack_own(yy, carry):
        pack(core, own0, yy)
        return carry

    firsts = []
    lax.fori_loop(0, NY, pack_away, 0)
    for f in range(2):
        firsts.append(send(p0.at[f], r0.at[f], cs.at[f], cr.at[f], partner))
    lax.fori_loop(0, NY, pack_own, 0)
    pl.semaphore_wait(ready2, 2)
    here = (y, z)
    ahead = (lambda d: at_yz(y + d, z), lambda d: at_yz(y, z + d))
    stage1 = ([], [])

    for f in range(2):
        firsts[f].wait_recv()
    for d in FAR_FIRST + (0,):
        for f in range(2):
            k = lax.rem(here[f] + d, 8)
            s0[f, k] = (own0[f, k] + r0[f, k].astype(jnp.float32)).astype(jnp.bfloat16)
            if d:
                stage1[f].append(
                    send(s0.at[f, k], r1.at[f, d - 1], s1s.at[f, d - 1], s1r.at[f, d - 1], ahead[f](d))
                )

    def back(n, carry):
        qgb[n] = lax.dot_general(
            wbuf[n], cand[n], (((0,), (0,)), ((), ())), preferred_element_type=jnp.float32
        ).astype(jnp.bfloat16)
        return carry

    lax.fori_loop(0, NX, back, 0)
    home = [
        pltpu.make_async_copy(qgb.at[g], qg_out.at[g], loc.at[7]),
        pltpu.make_async_copy(lossb.at[g], loss_out.at[g], loc.at[8]),
    ]
    backs = []
    for d in (2, 1, 3):
        dst = lax.rem(g + d, NX)
        for n, (src, out) in enumerate(((lossb, loss_out), (qgb, qg_out))):
            backs.append(send(src.at[dst], out.at[g], bs.at[d - 1, n], br.at[d - 1, n], x_peers[d - 1]))
    for copy in home:
        copy.start()

    stage2 = ([], [])
    for f in range(2):
        for copy in stage1[f]:
            copy.wait_recv()
        total = s0[f, here[f]].astype(jnp.float32)
        for d in range(7):
            total = total + r1[f, d].astype(jnp.float32)
        s1[f] = total.astype(jnp.bfloat16)
        for d in FAR_FIRST:
            k = lax.rem(here[1 - f] + d, 8)
            stage2[f].append(
                send(s1.at[f, k], r2.at[f, d - 1], s2s.at[f, d - 1], s2r.at[f, d - 1], ahead[1 - f](d))
            )
    for f in range(2):
        for copy in stage2[f]:
            copy.wait_recv()
        total = s1[f, here[1 - f]].astype(jnp.float32)
        for d in range(7):
            total = total + r2[f, d].astype(jnp.float32)
        fin[f] = total
    last = send(fin, rfin, fs, fr, partner)
    home.append(pltpu.make_async_copy(fin, fin_out, loc.at[9]))
    home[-1].start()
    for copy in home:
        copy.wait()
    for copy in backs:
        copy.wait_recv()
    last.wait_recv()
    for copy in sends:
        copy.wait_send()


def panf(ref):
    return ref.reshape(ref.shape[0] * ref.shape[1], *ref.shape[2:])


def output_kernel(qg, loss, fin, rfin, loss_out, qg_out, pg_out, qv, lv, fv, rv, lossv, pgv, sem):
    small = [
        pltpu.make_async_copy(src, dst, sem.at[n])
        for n, (src, dst) in enumerate(((loss, lv), (fin, fv), (rfin, rv)))
    ]
    taken = [pltpu.make_async_copy(qg.at[n], qv.at[n], sem.at[3 + n]) for n in range(NX)]
    for copy in small + taken:
        copy.start()
    given = []
    for copy in small:
        copy.wait()
    core = lax.rem(lax.axis_index("tower"), 2)
    for n in range(NX):
        lossv[n : n + 1, :] = lv[n].astype(jnp.bfloat16)
    for h in range(2):
        for f in range(2):
            tile = jnp.where(core == h, fv[f], rv[f])
            for k in range(4):
                rows = jnp.where(core == 0, tile[4 * k : 4 * k + 2], tile[4 * k + 2 : 4 * k + 4])
                pgv[4 * h + k, :, 128 * f : 128 * f + 128] = rows
    given = [
        pltpu.make_async_copy(lossv, loss_out, sem.at[7]),
        pltpu.make_async_copy(pgv, pg_out, sem.at[8]),
    ]
    for copy in given:
        copy.start()
    for n in range(NX):
        taken[n].wait()
        given.append(pltpu.make_async_copy(qv.at[n], qg_out.at[n], sem.at[9 + n]))
        given[-1].start()
    for copy in given:
        copy.wait()


def shards(queries, cluster_ids, positives, owner_map, panels, scales):
    count, rows, width = queries.shape
    slots, items = scales.shape
    blks = lax.axis_size("blk")
    sel = cluster_ids.shape[1]
    dma = pltpu.SemaphoreType.DMA
    hbm = pl.BlockSpec(memory_space=pltpu.HBM)
    vmem = pl.BlockSpec(memory_space=pltpu.VMEM)
    smem = pl.BlockSpec(memory_space=pltpu.SMEM)
    f32, bf16, i32 = jnp.float32, jnp.bfloat16, jnp.int32
    sds = jax.ShapeDtypeStruct
    vm = pltpu.VMEM

    qg, loss, fin, rfin = pl.pallas_call(
        main_kernel,
        out_shape=(
            sds((count, rows, width), bf16),
            sds((count, 1, rows), f32),
            sds((2, 16, 128), f32),
            sds((2, 16, 128), f32),
        ),
        in_specs=[smem] + [hbm] * 5,
        out_specs=(hbm,) * 4,
        scratch_shapes=[
            vm((count, rows, width), bf16),
            vm((count, 1, sel), i32),
            vm((count, count, rows), i32),
            vm((blks, slots, items, width), bf16),
            vm((blks, slots, items), bf16),
            pltpu.SMEM((count, 1, sel), i32),
            vm((blks * slots, items, 128), f32),
            vm((count, sel * items, width), bf16),
            vm((sel * items, rows), f32),
            vm((count, sel * items, rows), bf16),
            vm((count, sel + 1, items, width), f32),
            vm((count, 1, rows), f32),
            vm((count, rows, width), bf16),
            vm((count, 1, 128), i32),
            pltpu.SMEM((count, 1, 128), i32),
            vm((2, 8, 8, 16, 128), bf16),
            vm((2, 8, 8, 16, 128), f32),
            vm((2, 8, 8, 16, 128), bf16),
            vm((2, 8, 8, 16, 128), bf16),
            vm((2, 7, 8, 16, 128), bf16),
            vm((2, 8, 16, 128), bf16),
            vm((2, 7, 16, 128), bf16),
            vm((2, 16, 128), f32),
            dma((10,)), dma((3, 3)), dma((3, 3)),
            dma((7,)), dma((7,)), dma((7,)), dma((7,)),
            dma((8,)), dma((8,)), dma((8,)), dma((8,)), dma((15,)), dma((15,)),
            pltpu.SemaphoreType.REGULAR, pltpu.SemaphoreType.REGULAR,
            dma((2,)), dma((2,)), dma((2, 7)), dma((2, 7)), dma((2, 7)), dma((2, 7)),
            dma((3, 2)), dma((3, 2)), dma, dma,
        ],
        compiler_params=pltpu.CompilerParams(
            collective_id=0, has_side_effects=True, vmem_limit_bytes=60 << 20
        ),
        name="main",
    )(owner_map, queries, cluster_ids.reshape(count, 1, sel), positives, panels, scales)

    return pl.pallas_call(
        output_kernel,
        out_shape=(
            sds((count, rows), bf16),
            sds((count, rows, width), bf16),
            sds((slots, 2, width), f32),
        ),
        in_specs=[hbm] * 4,
        out_specs=(hbm,) * 3,
        scratch_shapes=[
            vm((count, rows, width), bf16), vm((count, 1, rows), f32),
            vm((2, 16, 128), f32), vm((2, 16, 128), f32),
            vm((count, rows), bf16), vm((slots, 2, width), f32), dma((13,)),
        ],
        compiler_params=pltpu.CompilerParams(vmem_limit_bytes=60 << 20),
        name="write",
    )(qg, loss, fin, rfin)


def solution(mesh):
    return jax.shard_map(
        shards,
        mesh=mesh,
        in_specs=(
            P(("tower", "group", "blk"), None, None),
            P(("tower", "group", "blk"), None),
            P(("tower", "group", "blk"), None),
            P("group", None),
            P(("group", "blk"), None, None),
            P(("group", "blk"), None),
        ),
        out_specs=(
            P(("tower", "group", "blk"), None),
            P(("tower", "group", "blk"), None, None),
            P(("group", "blk"), "tower", None),
        ),
        check_vma=False,
    )
```

```python
import jax
import jax.numpy as jnp
from jax import lax
from jax.experimental import pallas as pl
from jax.experimental.pallas import tpu as pltpu
from jax.sharding import PartitionSpec as P

MESH = pl.DeviceIdType.MESH
NX, NY, NZ = 4, 8, 8
INWARD = (4, 3, 5, 2, 6, 1, 7)


def remote(src, dst, send, recv, peer):
    return pltpu.make_async_remote_copy(
        src_ref=src, dst_ref=dst, send_sem=send, recv_sem=recv, device_id=peer, device_id_type=MESH
    )


def signal(sem, peer):
    pl.semaphore_signal(sem, inc=1, device_id=peer, device_id_type=MESH)


def score_block(n, row, slots, q_ref, pos_ref, pan_ref, tab, cand, sbuf, wbuf, gbuf, loss_ref):
    items, sel, rows = 16, len(slots), q_ref.shape[1]
    sub = lax.broadcasted_iota(jnp.int32, (items, rows), 0)

    def wide(slot):
        one = tab[slot]
        return jnp.concatenate([one] * (rows // 128), axis=1)

    for j in range(sel):
        cand[n, pl.ds(items * j, items), :] = pan_ref[slots[j]]
    q = q_ref[n]
    sbuf[...] = lax.dot_general(
        cand[n], q, (((1,), (1,)), ((), ())), preferred_element_type=jnp.float32
    )
    peak = jnp.full((items, rows), -jnp.inf, jnp.float32)
    for j in range(sel):
        at = pl.ds(items * j, items)
        s = sbuf[at, :] * wide(slots[j])
        sbuf[at, :] = s
        peak = jnp.maximum(peak, s)
    peak = jnp.max(peak, axis=0, keepdims=True)
    pos = pos_ref[n, pl.ds(row, 1), :]
    rel = jnp.broadcast_to(pos, (items, rows)) - sub
    total = jnp.zeros((items, rows), jnp.float32)
    picked = jnp.zeros((items, rows), jnp.float32)
    for j in range(sel):
        at = pl.ds(items * j, items)
        s = sbuf[at, :]
        picked = jnp.where(rel == items * j, s, picked)
        e = jnp.exp(s - peak)
        sbuf[at, :] = e
        total = total + e
    total = jnp.sum(total, axis=0, keepdims=True)
    picked = jnp.sum(picked, axis=0, keepdims=True)
    loss_ref[n] = peak + jnp.log(total) - picked
    inverse = 1.0 / total
    for j in range(sel):
        at = pl.ds(items * j, items)
        chance = sbuf[at, :] * inverse
        w = jnp.where(rel == items * j, chance - 1.0, chance) * wide(slots[j])
        wbuf[n, at, :] = w.astype(jnp.bfloat16)
    grad = jnp.dot(wbuf[n], q, preferred_element_type=jnp.float32)
    gbuf[n, pl.ds(0, sel)] = grad.reshape(sel, items, grad.shape[1])


def main_kernel(
    own_map, q, ids, pos, pan, sc,
    qg_out, loss_out, pg_out,
    owner, lbuf, qo, ido, poso, pano, sco, ids_s, tab, cand, sbuf, wbuf, gbuf, lossb, qgb, inv_v, inv_s,
    p0, own0, r0, s0, r1, s1, r2,
    loc, xs, xr, ys, yr, yss, yrs, zs, zr, zss, zrs, ps, pr, ready1, ready2,
    cs, cr, s1s, s1r, s2s, s2r, bs, br,
):
    t, g, b = lax.axis_index("tower"), lax.axis_index("group"), lax.axis_index("blk")
    core, y, zl = lax.rem(t, 2), lax.div(b, 2), lax.rem(b, 2)
    z = 2 * lax.div(t, 2) + zl
    step = 1 - 2 * core

    def at_yz(yy, zz, c=core):
        yy, zz = lax.rem(yy + NY, NY), lax.rem(zz + NZ, NZ)
        return (2 * lax.div(zz, 2) + c, g, 2 * yy + lax.rem(zz, 2))

    partner = (t + step, g, b)
    x_peers = [(t, lax.rem(g + d, NX), b) for d in range(1, NX)]
    z_to, z_from = at_yz(y, z + step), at_yz(y, z - step)

    local = [
        pltpu.make_async_copy(pan, pano.at[b], loc.at[0]),
        pltpu.make_async_copy(sc, sco.at[b], loc.at[1]),
        pltpu.make_async_copy(own_map, owner, loc.at[2]),
    ]
    own = [
        pltpu.make_async_copy(ids.at[g], ido.at[g], xr.at[0, 0]),
        pltpu.make_async_copy(pos, poso.at[g], xr.at[0, 1]),
        pltpu.make_async_copy(q.at[g], qo.at[g], xr.at[0, 2]),
    ]
    near = [at_yz(y + d, z) for d in (2, -2)] + x_peers
    near += [at_yz(y + d, z) for d in (1, -1)] + [z_to, z_from, partner]
    barrier = pltpu.get_barrier_semaphore()
    for d in (2 * step, 1, -1):
        signal(barrier, at_yz(y - d, z - step))
    for peer in near:
        signal(barrier, peer)
    for copy in local + own:
        copy.start()
    pl.semaphore_wait(barrier, len(near) + 3)

    half = pl.ds(core * 4, 4)
    sends = []

    def send(src, dst, s, r, peer):
        copy = remote(src, dst, s, r, peer)
        copy.start()
        sends.append(copy)
        return copy

    y_in, z_in, p_in = {}, {}, []

    def y_send(d, src_blk, panel, scale, peer):
        y_in[d] = [
            send(panel, pano.at[src_blk, half], ys.at[d - 1], yr.at[d - 1], peer),
            send(scale, sco.at[src_blk], yss.at[d - 1], yrs.at[d - 1], peer),
        ]

    def z_send(d, src_blk, panel, scale, peer):
        z_in[d] = [
            send(panel, pano.at[src_blk, half], zs.at[d], zr.at[d], peer),
            send(scale, sco.at[src_blk], zss.at[d], zrs.at[d], peer),
        ]

    def p_send(src_blk):
        k = len(p_in)
        piece = pano.at[src_blk, half]
        p_in.append(send(piece, piece, ps.at[k], pr.at[k], partner))

    def blk_at(d, side):
        return 2 * lax.rem(y - d + NY, NY) + side

    for d in (2, 6, 1, 7):
        y_send(d, b, pan.at[half], sc, at_yz(y + d, z))
    z_send(0, b, pan.at[half], sc, z_to)
    for peer in (z_to, z_from):
        signal(ready1, peer)
    ids_in = []
    for d in (1, 3, 2):
        dst = lax.rem(g + d, NX)
        for n, (src, out) in enumerate(
            ((ids.at[dst], ido.at[g]), (pos, poso.at[g]), (q.at[dst], qo.at[g]))
        ):
            copy = send(src, out, xs.at[d - 1, n], xr.at[d, n], x_peers[d - 1])
            if n == 0:
                ids_in.append(copy)

    def take_y(d):
        for copy in y_in[d]:
            copy.wait_recv()

    def take_z(d):
        for copy in z_in[d]:
            copy.wait_recv()
        p_send(blk_at(d, 1 - zl))

    def pass_on(d, src, dy):
        panel, scale = pano.at[src, half], sco.at[src]
        z_send(d, src, panel, scale, at_yz(y + dy, z + step))
        y_send(d, src, panel, scale, at_yz(y + dy, z))

    def spread(d):
        src = blk_at(d, zl)
        z_send(d, src, pano.at[src, half], sco.at[src], z_to)
        p_send(src)

    take_y(2)
    pass_on(3, blk_at(2, zl), 1)
    take_y(6)
    pass_on(5, blk_at(6, zl), -1)
    pass_on(4, 2 * lax.rem(y - 2 * step + NY, NY) + zl, 2 * step)
    for d in (1, 7):
        take_y(d)
    for d in (2, 6, 1, 7):
        spread(d)
    take_z(0)
    pl.semaphore_wait(ready1, 2)
    for d in (2, -2):
        signal(ready2, at_yz(y, z + d))
    for d in (3, 5, 4):
        take_y(d)
        p_send(blk_at(d, zl))
    for d in (1, 7, 2, 6, 3, 5, 4):
        take_z(d)
    for copy in local + own[:1]:
        copy.wait()
    for copy in ids_in:
        copy.wait_recv()
    to_smem = pltpu.make_async_copy(ido, ids_s, loc.at[3])
    to_smem.start()

    items = 16
    eye = (
        lax.broadcasted_iota(jnp.int32, (items, items), 0)
        == lax.broadcasted_iota(jnp.int32, (items, items), 1)
    ).astype(jnp.float32)
    for n in range(sco.shape[0]):
        part = sco[n].astype(jnp.float32)
        column = jnp.sum(part[:, None, :] * eye[None], axis=2, keepdims=True)
        tab[pl.ds(8 * n, 8)] = jnp.broadcast_to(column, (8, items, 128))
    sel = ids_s.shape[2]
    for n in range(NX):
        gbuf[n, sel] = jnp.zeros(gbuf.shape[2:], jnp.float32)
    for copy in p_in:
        copy.wait_recv()
    to_smem.wait()
    lane = lax.broadcasted_iota(jnp.int32, (1, 128), 1)

    def block(k, carry):
        d = k + lax.div(k, 2) * (5 - 2 * k)
        n = lax.rem(g - d + NX, NX)
        pltpu.make_async_copy(pos, poso.at[n], xr.at[d, 1]).wait()
        pltpu.make_async_copy(q.at[n], qo.at[n], xr.at[d, 2]).wait()
        slots = [owner[0, ids_s[n, 0, j]] for j in range(sel)]
        where = jnp.full((1, 128), sel, jnp.int32)
        for j in range(sel):
            where = jnp.where(lane == slots[j], j, where)
        inv_v[n] = where
        score_block(n, g, slots, qo, poso, panf(pano), tab, cand, sbuf, wbuf, gbuf, lossb)
        return carry

    lax.fori_loop(0, NX, block, 0)
    inv_copy = pltpu.make_async_copy(inv_v, inv_s, loc.at[4])
    inv_copy.start()
    inv_copy.wait()

    low = lax.broadcasted_iota(jnp.int32, (8, 256), 0) < 4

    def pack(h, out, yy):
        for side in range(2):
            base = (2 * yy + side) * 8 + 4 * h
            rows = []
            for k in range(4):
                total = gbuf[0, inv_s[0, 0, base + k]]
                for n in range(1, NX):
                    total = total + gbuf[n, inv_s[n, 0, base + k]]
                rows.append(total)
            for v in range(2):
                tiles = ([], [])
                for sp in range(2):
                    a = rows[2 * sp][8 * v : 8 * v + 8]
                    c = rows[2 * sp + 1][8 * v : 8 * v + 8]
                    tiles[0].append(jnp.where(low, a, pltpu.roll(c, 4, axis=0)))
                    tiles[1].append(jnp.where(low, pltpu.roll(a, 4, axis=0), c))
                for k in range(2):
                    zz = 2 * (2 * v + k) + side
                    tile = jnp.concatenate(tiles[k], axis=0).astype(out.dtype)
                    out[0, yy, zz] = tile[:, :128]
                    out[1, zz, yy] = tile[:, 128:]

    def pack_away(yy, carry):
        pack(1 - core, p0, yy)
        return carry

    def pack_own(yy, carry):
        pack(core, own0, yy)
        return carry

    firsts = []
    pl.semaphore_wait(ready2, 2)
    lax.fori_loop(0, NY, pack_away, 0)
    for f in range(2):
        firsts.append(send(p0.at[f], r0.at[f], cs.at[f], cr.at[f], partner))
    lax.fori_loop(0, NY, pack_own, 0)
    here = (y, z)
    ahead = (lambda d: at_yz(y + d, z), lambda d: at_yz(y, z + d))
    stage1 = ([], [])

    for f in range(2):
        firsts[f].wait_recv()
    for d in INWARD + (0,):
        for f in range(2):
            k = lax.rem(here[f] + d, 8)
            s0[f, k] = (own0[f, k] + r0[f, k].astype(jnp.float32)).astype(jnp.bfloat16)
            if d:
                stage1[f].append(
                    send(s0.at[f, k], r1.at[f, d - 1], s1s.at[f, d - 1], s1r.at[f, d - 1], ahead[f](d))
                )

    def back(n, carry):
        qgb[n] = lax.dot_general(
            wbuf[n], cand[n], (((0,), (0,)), ((), ())), preferred_element_type=jnp.float32
        ).astype(jnp.bfloat16)
        return carry

    lax.fori_loop(0, NX, back, 0)
    home = [
        pltpu.make_async_copy(qgb.at[g], qg_out.at[g], loc.at[5]),
        pltpu.make_async_copy(lossb.at[g], lbuf.at[g], loc.at[6]),
    ]
    backs = []
    for d in (2, 1, 3):
        dst = lax.rem(g + d, NX)
        for n, (src, out) in enumerate(((lossb, lbuf), (qgb, qg_out))):
            backs.append(send(src.at[dst], out.at[g], bs.at[d - 1, n], br.at[d - 1, n], x_peers[d - 1]))
    for copy in home:
        copy.start()

    stage2 = []
    for f in range(2):
        for copy in stage1[f]:
            copy.wait_recv()
        total = s0[f, here[f]].astype(jnp.float32)
        for d in range(7):
            total = total + r1[f, d].astype(jnp.float32)
        s1[f] = total.astype(jnp.bfloat16)
        for d in INWARD + (0,):
            piece = s1.at[f, lax.rem(here[1 - f] + d, 8)]
            for other in (1, 0) if d else (1,):
                c = core + other * step
                peer = at_yz(y, z + d, c) if f == 0 else at_yz(y + d, z, c)
                stage2.append(
                    send(piece, r2.at[core, f, d], s2s.at[other, f, d], s2r.at[other, f, d], peer)
                )
    r2[core, 0, 0] = s1[0, z]
    r2[core, 1, 0] = s1[1, y]
    for copy in home:
        copy.wait()
    for copy in backs:
        copy.wait_recv()
    for n in range(NX):
        loss_out[n : n + 1, :] = lbuf[n].astype(jnp.bfloat16)
    for copy in stage2:
        copy.wait_recv()
    for h in range(2):
        for f in range(2):
            tile = r2[h, f, 0].astype(jnp.float32)
            for d in range(1, 8):
                tile = tile + r2[h, f, d].astype(jnp.float32)
            for k in range(4):
                rows = jnp.where(core == 0, tile[4 * k : 4 * k + 2], tile[4 * k + 2 : 4 * k + 4])
                pg_out[4 * h + k, :, 128 * f : 128 * f + 128] = rows
    for copy in sends:
        copy.wait_send()


def panf(ref):
    return ref.reshape(ref.shape[0] * ref.shape[1], *ref.shape[2:])


def output_kernel(loss, qg, pg, loss_out, qg_out, pg_out, sem):
    copies = [
        pltpu.make_async_copy(src, dst, sem.at[n])
        for n, (src, dst) in enumerate(((qg, qg_out), (loss, loss_out), (pg, pg_out)))
    ]
    for copy in copies:
        copy.start()
    for copy in copies:
        copy.wait()


def shards(queries, cluster_ids, positives, owner_map, panels, scales):
    count, rows, width = queries.shape
    slots, items = scales.shape
    blks = lax.axis_size("blk")
    sel = cluster_ids.shape[1]
    dma = pltpu.SemaphoreType.DMA
    hbm = pl.BlockSpec(memory_space=pltpu.HBM)
    vmem = pl.BlockSpec(memory_space=pltpu.VMEM)
    smem = pl.BlockSpec(memory_space=pltpu.SMEM)
    f32, bf16, i32 = jnp.float32, jnp.bfloat16, jnp.int32
    sds = jax.ShapeDtypeStruct
    vm = pltpu.VMEM

    args = (owner_map, queries, cluster_ids.reshape(count, 1, sel), positives, panels, scales)
    outs = (
        sds((count, rows), bf16),
        sds((count, rows, width), bf16),
        sds((slots, 2, width), f32),
    )
    qg, loss, pg = pl.pallas_call(
        main_kernel,
        out_shape=(outs[1], outs[0], outs[2]),
        in_specs=[hbm] * 6,
        out_specs=(vmem,) * 3,
        scratch_shapes=[
            pltpu.SMEM(owner_map.shape, i32),
            vm((count, 1, rows), f32),
            vm((count, rows, width), bf16),
            vm((count, 1, sel), i32),
            vm((count, count, rows), i32),
            vm((blks, slots, items, width), bf16),
            vm((blks, slots, items), bf16),
            pltpu.SMEM((count, 1, sel), i32),
            vm((blks * slots, items, 128), f32),
            vm((count, sel * items, width), bf16),
            vm((sel * items, rows), f32),
            vm((count, sel * items, rows), bf16),
            vm((count, sel + 1, items, width), f32),
            vm((count, 1, rows), f32),
            vm((count, rows, width), bf16),
            vm((count, 1, 128), i32),
            pltpu.SMEM((count, 1, 128), i32),
            vm((2, 8, 8, 16, 128), bf16),
            vm((2, 8, 8, 16, 128), f32),
            vm((2, 8, 8, 16, 128), bf16),
            vm((2, 8, 8, 16, 128), bf16),
            vm((2, 7, 8, 16, 128), bf16),
            vm((2, 8, 16, 128), bf16),
            vm((2, 2, 8, 16, 128), bf16),
            dma((7,)), dma((3, 3)), dma((4, 3)),
            dma((7,)), dma((7,)), dma((7,)), dma((7,)),
            dma((8,)), dma((8,)), dma((8,)), dma((8,)), dma((15,)), dma((15,)),
            pltpu.SemaphoreType.REGULAR, pltpu.SemaphoreType.REGULAR,
            dma((2,)), dma((2,)), dma((2, 7)), dma((2, 7)), dma((2, 2, 8)), dma((2, 2, 8)),
            dma((3, 2)), dma((3, 2)),
        ],
        compiler_params=pltpu.CompilerParams(
            collective_id=0, has_side_effects=True, vmem_limit_bytes=40 << 20
        ),
        name="main",
    )(*[pltpu.with_memory_space_constraint(arg, pltpu.HBM) for arg in args])

    return pl.pallas_call(
        output_kernel,
        out_shape=outs,
        in_specs=[vmem] * 3,
        out_specs=(hbm,) * 3,
        scratch_shapes=[dma((3,))],
        compiler_params=pltpu.CompilerParams(vmem_limit_bytes=4 << 20),
        name="write",
    )(loss, qg, pg)


def solution(mesh):
    return jax.shard_map(
        shards,
        mesh=mesh,
        in_specs=(
            P(("tower", "group", "blk"), None, None),
            P(("tower", "group", "blk"), None),
            P(("tower", "group", "blk"), None),
            P("group", None),
            P(("group", "blk"), None, None),
            P(("group", "blk"), None),
        ),
        out_specs=(
            P(("tower", "group", "blk"), None),
            P(("tower", "group", "blk"), None, None),
            P(("group", "blk"), "tower", None),
        ),
        check_vma=False,
    )
```

```python
import jax
import jax.numpy as jnp
from jax import lax
from jax.experimental import pallas as pl
from jax.experimental.pallas import tpu as pltpu
from jax.sharding import PartitionSpec as P

MESH = pl.DeviceIdType.MESH
NX, NY, NZ = 4, 8, 8
INWARD = (4, 3, 5, 2, 6, 1, 7)


def remote(src, dst, send, recv, peer):
    return pltpu.make_async_remote_copy(
        src_ref=src, dst_ref=dst, send_sem=send, recv_sem=recv, device_id=peer, device_id_type=MESH
    )


def signal(sem, peer):
    pl.semaphore_signal(sem, inc=1, device_id=peer, device_id_type=MESH)


def score_block(n, row, slots, q_ref, pos_ref, pan_ref, tab, cand, sbuf, wbuf, gbuf, loss_ref):
    items, sel, rows = 16, len(slots), q_ref.shape[1]
    sub = lax.broadcasted_iota(jnp.int32, (items, rows), 0)

    def wide(slot):
        one = tab[slot]
        return jnp.concatenate([one] * (rows // 128), axis=1)

    for j in range(sel):
        cand[n, pl.ds(items * j, items), :] = pan_ref[slots[j]]
    q = q_ref[n]
    sbuf[...] = lax.dot_general(
        cand[n], q, (((1,), (1,)), ((), ())), preferred_element_type=jnp.float32
    )
    peak = jnp.full((items, rows), -jnp.inf, jnp.float32)
    for j in range(sel):
        at = pl.ds(items * j, items)
        s = sbuf[at, :] * wide(slots[j])
        sbuf[at, :] = s
        peak = jnp.maximum(peak, s)
    peak = jnp.max(peak, axis=0, keepdims=True)
    pos = pos_ref[n, pl.ds(row, 1), :]
    rel = jnp.broadcast_to(pos, (items, rows)) - sub
    total = jnp.zeros((items, rows), jnp.float32)
    picked = jnp.zeros((items, rows), jnp.float32)
    for j in range(sel):
        at = pl.ds(items * j, items)
        s = sbuf[at, :]
        picked = jnp.where(rel == items * j, s, picked)
        e = jnp.exp(s - peak)
        sbuf[at, :] = e
        total = total + e
    total = jnp.sum(total, axis=0, keepdims=True)
    picked = jnp.sum(picked, axis=0, keepdims=True)
    loss_ref[n] = peak + jnp.log(total) - picked
    inverse = 1.0 / total
    for j in range(sel):
        at = pl.ds(items * j, items)
        chance = sbuf[at, :] * inverse
        w = jnp.where(rel == items * j, chance - 1.0, chance) * wide(slots[j])
        wbuf[n, at, :] = w.astype(jnp.bfloat16)
    grad = jnp.dot(wbuf[n], q, preferred_element_type=jnp.float32)
    gbuf[n, pl.ds(0, sel)] = grad.reshape(sel, items, grad.shape[1])


def main_kernel(
    own_map, q, ids, pos, pan, sc,
    qg_out, loss_out, pg_out,
    owner, lbuf, qo, ido, poso, pano, sco, ids_s, tab, cand, sbuf, wbuf, gbuf, lossb, qgb, inv_v, inv_s,
    p0, own0, r0, s0, r1, s1, r2,
    loc, xs, xr, ys, yr, yss, yrs, zs, zr, zss, zrs, ps, pr, ready1, ready2,
    cs, cr, s1s, s1r, s2s, s2r, bs, br,
):
    t, g, b = lax.axis_index("tower"), lax.axis_index("group"), lax.axis_index("blk")
    core, y, zl = lax.rem(t, 2), lax.div(b, 2), lax.rem(b, 2)
    z = 2 * lax.div(t, 2) + zl
    step = 1 - 2 * core

    def at_yz(yy, zz, c=core):
        yy, zz = lax.rem(yy + NY, NY), lax.rem(zz + NZ, NZ)
        return (2 * lax.div(zz, 2) + c, g, 2 * yy + lax.rem(zz, 2))

    partner = (t + step, g, b)
    x_peers = [(t, lax.rem(g + d, NX), b) for d in range(1, NX)]
    z_to, z_from = at_yz(y, z + step), at_yz(y, z - step)

    local = [
        pltpu.make_async_copy(pan, pano.at[b], loc.at[0]),
        pltpu.make_async_copy(sc, sco.at[b], loc.at[1]),
        pltpu.make_async_copy(own_map, owner, loc.at[2]),
    ]
    own = [
        pltpu.make_async_copy(ids.at[g], ido.at[g], xr.at[0, 0]),
        pltpu.make_async_copy(pos, poso.at[g], xr.at[0, 1]),
        pltpu.make_async_copy(q.at[g], qo.at[g], xr.at[0, 2]),
    ]
    near = [at_yz(y + d, z) for d in (2, -2)] + x_peers
    near += [at_yz(y + d, z) for d in (1, -1)] + [z_to, z_from, partner]
    barrier = pltpu.get_barrier_semaphore()
    for d in (2 * step, 1, -1):
        signal(barrier, at_yz(y - d, z - step))
    for peer in near:
        signal(barrier, peer)
    for copy in local + own:
        copy.start()
    pl.semaphore_wait(barrier, len(near) + 3)

    half = pl.ds(core * 4, 4)
    sends = []

    def send(src, dst, s, r, peer):
        copy = remote(src, dst, s, r, peer)
        copy.start()
        sends.append(copy)
        return copy

    y_in, z_in, p_in = {}, {}, []

    def y_send(d, src_blk, panel, scale, peer):
        y_in[d] = [
            send(panel, pano.at[src_blk, half], ys.at[d - 1], yr.at[d - 1], peer),
            send(scale, sco.at[src_blk], yss.at[d - 1], yrs.at[d - 1], peer),
        ]

    def z_send(d, src_blk, panel, scale, peer):
        z_in[d] = [
            send(panel, pano.at[src_blk, half], zs.at[d], zr.at[d], peer),
            send(scale, sco.at[src_blk], zss.at[d], zrs.at[d], peer),
        ]

    def p_send(src_blk):
        k = len(p_in)
        piece = pano.at[src_blk, half]
        p_in.append(send(piece, piece, ps.at[k], pr.at[k], partner))

    def blk_at(d, side):
        return 2 * lax.rem(y - d + NY, NY) + side

    for d in (2, 6, 1, 7):
        y_send(d, b, pan.at[half], sc, at_yz(y + d, z))
    z_send(0, b, pan.at[half], sc, z_to)
    for peer in (z_to, z_from):
        signal(ready1, peer)
    ids_in = []
    for d in (1, 3, 2):
        dst = lax.rem(g + d, NX)
        for n, (src, out) in enumerate(
            ((ids.at[dst], ido.at[g]), (pos, poso.at[g]), (q.at[dst], qo.at[g]))
        ):
            copy = send(src, out, xs.at[d - 1, n], xr.at[d, n], x_peers[d - 1])
            if n == 0:
                ids_in.append(copy)

    items = 16
    eye = (
        lax.broadcasted_iota(jnp.int32, (items, items), 0)
        == lax.broadcasted_iota(jnp.int32, (items, items), 1)
    ).astype(jnp.float32)

    def scale_tiles(src):
        part = sco[src].astype(jnp.float32)
        column = jnp.sum(part[:, None, :] * eye[None], axis=2, keepdims=True)
        tab[pl.ds(8 * src, 8)] = jnp.broadcast_to(column, (8, items, 128))

    def take_y(d):
        for copy in y_in[d]:
            copy.wait_recv()

    def take_z(d):
        for copy in z_in[d]:
            copy.wait_recv()
        p_send(blk_at(d, 1 - zl))
        scale_tiles(blk_at(d, 1 - zl))

    def pass_on(d, src, dy):
        panel, scale = pano.at[src, half], sco.at[src]
        z_send(d, src, panel, scale, at_yz(y + dy, z + step))
        y_send(d, src, panel, scale, at_yz(y + dy, z))

    def spread(d):
        src = blk_at(d, zl)
        z_send(d, src, pano.at[src, half], sco.at[src], z_to)
        p_send(src)

    take_y(2)
    pass_on(3, blk_at(2, zl), 1)
    take_y(6)
    pass_on(5, blk_at(6, zl), -1)
    pass_on(4, 2 * lax.rem(y - 2 * step + NY, NY) + zl, 2 * step)
    for d in (1, 7):
        take_y(d)
    for d in (2, 6, 1, 7):
        spread(d)
    sel = ids_s.shape[2]
    for n in range(NX):
        gbuf[n, sel] = jnp.zeros(gbuf.shape[2:], jnp.float32)
    for copy in local:
        copy.wait()
    for d in (0, 2, 6, 1, 7):
        scale_tiles(blk_at(d, zl))
    take_z(0)
    pl.semaphore_wait(ready1, 2)
    for d in (2, -2):
        signal(ready2, at_yz(y, z + d))
    for d in (3, 5, 4):
        take_y(d)
        p_send(blk_at(d, zl))
        scale_tiles(blk_at(d, zl))
    own[0].wait()
    for copy in ids_in:
        copy.wait_recv()
    to_smem = pltpu.make_async_copy(ido, ids_s, loc.at[3])
    to_smem.start()
    for d in (1, 7, 2, 6, 3, 5, 4):
        take_z(d)

    for copy in p_in:
        copy.wait_recv()
    to_smem.wait()
    lane = lax.broadcasted_iota(jnp.int32, (1, 128), 1)

    def block(k, carry):
        d = k + lax.div(k, 2) * (5 - 2 * k)
        n = lax.rem(g - d + NX, NX)
        pltpu.make_async_copy(pos, poso.at[n], xr.at[d, 1]).wait()
        pltpu.make_async_copy(q.at[n], qo.at[n], xr.at[d, 2]).wait()
        slots = [owner[0, ids_s[n, 0, j]] for j in range(sel)]
        where = jnp.full((1, 128), sel, jnp.int32)
        for j in range(sel):
            where = jnp.where(lane == slots[j], j, where)
        inv_v[n] = where
        score_block(n, g, slots, qo, poso, panf(pano), tab, cand, sbuf, wbuf, gbuf, lossb)
        return carry

    lax.fori_loop(0, NX, block, 0)
    inv_copy = pltpu.make_async_copy(inv_v, inv_s, loc.at[4])
    inv_copy.start()
    inv_copy.wait()

    low = lax.broadcasted_iota(jnp.int32, (8, 256), 0) < 4

    def pack(h, out, yy):
        for side in range(2):
            base = (2 * yy + side) * 8 + 4 * h
            rows = []
            for k in range(4):
                total = gbuf[0, inv_s[0, 0, base + k]]
                for n in range(1, NX):
                    total = total + gbuf[n, inv_s[n, 0, base + k]]
                rows.append(total)
            for v in range(2):
                tiles = ([], [])
                for sp in range(2):
                    a = rows[2 * sp][8 * v : 8 * v + 8]
                    c = rows[2 * sp + 1][8 * v : 8 * v + 8]
                    tiles[0].append(jnp.where(low, a, pltpu.roll(c, 4, axis=0)))
                    tiles[1].append(jnp.where(low, pltpu.roll(a, 4, axis=0), c))
                for k in range(2):
                    zz = 2 * (2 * v + k) + side
                    tile = jnp.concatenate(tiles[k], axis=0).astype(out.dtype)
                    out[0, yy, zz] = tile[:, :128]
                    out[1, zz, yy] = tile[:, 128:]

    def pack_away(yy, carry):
        pack(1 - core, p0, yy)
        return carry

    def pack_own(yy, carry):
        pack(core, own0, yy)
        return carry

    firsts = []
    pl.semaphore_wait(ready2, 2)
    lax.fori_loop(0, NY // 2, pack_away, 0)
    for f in range(2):
        part = (f, pl.ds(0, 4)) if f == 0 else (f, slice(None), pl.ds(0, 4))
        firsts.append(send(p0.at[part], r0.at[part], cs.at[f], cr.at[f], partner))
    lax.fori_loop(NY // 2, NY, pack_away, 0)
    for f in range(2):
        part = (f, pl.ds(4, 4)) if f == 0 else (f, slice(None), pl.ds(4, 4))
        firsts.append(send(p0.at[part], r0.at[part], cs.at[2 + f], cr.at[2 + f], partner))
    lax.fori_loop(0, NY, pack_own, 0)
    here = (y, z)
    ahead = (lambda d: at_yz(y + d, z), lambda d: at_yz(y, z + d))
    stage1 = ([], [])

    for copy in firsts:
        copy.wait_recv()
    for d in INWARD + (0,):
        for f in range(2):
            k = lax.rem(here[f] + d, 8)
            s0[f, k] = (own0[f, k] + r0[f, k].astype(jnp.float32)).astype(jnp.bfloat16)
            if d:
                stage1[f].append(
                    send(s0.at[f, k], r1.at[f, d - 1], s1s.at[f, d - 1], s1r.at[f, d - 1], ahead[f](d))
                )

    def back(n, carry):
        qgb[n] = lax.dot_general(
            wbuf[n], cand[n], (((0,), (0,)), ((), ())), preferred_element_type=jnp.float32
        ).astype(jnp.bfloat16)
        return carry

    lax.fori_loop(0, NX, back, 0)
    home = [
        pltpu.make_async_copy(qgb.at[g], qg_out.at[g], loc.at[5]),
        pltpu.make_async_copy(lossb.at[g], lbuf.at[g], loc.at[6]),
    ]
    backs = []
    for d in (2, 1, 3):
        dst = lax.rem(g + d, NX)
        for n, (src, out) in enumerate(((lossb, lbuf), (qgb, qg_out))):
            backs.append(send(src.at[dst], out.at[g], bs.at[d - 1, n], br.at[d - 1, n], x_peers[d - 1]))
    for copy in home:
        copy.start()

    stage2 = []
    for f in range(2):
        for copy in stage1[f]:
            copy.wait_recv()
        total = s0[f, here[f]].astype(jnp.float32)
        for d in range(7):
            total = total + r1[f, d].astype(jnp.float32)
        s1[f] = total.astype(jnp.bfloat16)
        for d in INWARD + (0,):
            piece = s1.at[f, lax.rem(here[1 - f] + d, 8)]
            for other in (1, 0) if d else (1,):
                c = core + other * step
                peer = at_yz(y, z + d, c) if f == 0 else at_yz(y + d, z, c)
                stage2.append(
                    send(piece, r2.at[core, f, d], s2s.at[other, f, d], s2r.at[other, f, d], peer)
                )
    r2[core, 0, 0] = s1[0, z]
    r2[core, 1, 0] = s1[1, y]
    for copy in home:
        copy.wait()
    for copy in backs:
        copy.wait_recv()
    for n in range(NX):
        loss_out[n : n + 1, :] = lbuf[n].astype(jnp.bfloat16)
    for copy in stage2:
        copy.wait_recv()
    for h in range(2):
        for f in range(2):
            tile = r2[h, f, 0].astype(jnp.float32)
            for d in range(1, 8):
                tile = tile + r2[h, f, d].astype(jnp.float32)
            for k in range(4):
                rows = jnp.where(core == 0, tile[4 * k : 4 * k + 2], tile[4 * k + 2 : 4 * k + 4])
                pg_out[4 * h + k, :, 128 * f : 128 * f + 128] = rows
    for copy in sends:
        copy.wait_send()


def panf(ref):
    return ref.reshape(ref.shape[0] * ref.shape[1], *ref.shape[2:])


def output_kernel(loss, qg, pg, loss_out, qg_out, pg_out, sem):
    copies = [
        pltpu.make_async_copy(src, dst, sem.at[n])
        for n, (src, dst) in enumerate(((qg, qg_out), (loss, loss_out), (pg, pg_out)))
    ]
    for copy in copies:
        copy.start()
    for copy in copies:
        copy.wait()


def shards(queries, cluster_ids, positives, owner_map, panels, scales):
    count, rows, width = queries.shape
    slots, items = scales.shape
    blks = lax.axis_size("blk")
    sel = cluster_ids.shape[1]
    dma = pltpu.SemaphoreType.DMA
    hbm = pl.BlockSpec(memory_space=pltpu.HBM)
    vmem = pl.BlockSpec(memory_space=pltpu.VMEM)
    smem = pl.BlockSpec(memory_space=pltpu.SMEM)
    f32, bf16, i32 = jnp.float32, jnp.bfloat16, jnp.int32
    sds = jax.ShapeDtypeStruct
    vm = pltpu.VMEM

    args = (owner_map, queries, cluster_ids.reshape(count, 1, sel), positives, panels, scales)
    outs = (
        sds((count, rows), bf16),
        sds((count, rows, width), bf16),
        sds((slots, 2, width), f32),
    )
    qg, loss, pg = pl.pallas_call(
        main_kernel,
        out_shape=(outs[1], outs[0], outs[2]),
        in_specs=[hbm] * 6,
        out_specs=(vmem,) * 3,
        scratch_shapes=[
            pltpu.SMEM(owner_map.shape, i32),
            vm((count, 1, rows), f32),
            vm((count, rows, width), bf16),
            vm((count, 1, sel), i32),
            vm((count, count, rows), i32),
            vm((blks, slots, items, width), bf16),
            vm((blks, slots, items), bf16),
            pltpu.SMEM((count, 1, sel), i32),
            vm((blks * slots, items, 128), f32),
            vm((count, sel * items, width), bf16),
            vm((sel * items, rows), f32),
            vm((count, sel * items, rows), bf16),
            vm((count, sel + 1, items, width), f32),
            vm((count, 1, rows), f32),
            vm((count, rows, width), bf16),
            vm((count, 1, 128), i32),
            pltpu.SMEM((count, 1, 128), i32),
            vm((2, 8, 8, 16, 128), bf16),
            vm((2, 8, 8, 16, 128), f32),
            vm((2, 8, 8, 16, 128), bf16),
            vm((2, 8, 8, 16, 128), bf16),
            vm((2, 7, 8, 16, 128), bf16),
            vm((2, 8, 16, 128), bf16),
            vm((2, 2, 8, 16, 128), bf16),
            dma((7,)), dma((3, 3)), dma((4, 3)),
            dma((7,)), dma((7,)), dma((7,)), dma((7,)),
            dma((8,)), dma((8,)), dma((8,)), dma((8,)), dma((15,)), dma((15,)),
            pltpu.SemaphoreType.REGULAR, pltpu.SemaphoreType.REGULAR,
            dma((4,)), dma((4,)), dma((2, 7)), dma((2, 7)), dma((2, 2, 8)), dma((2, 2, 8)),
            dma((3, 2)), dma((3, 2)),
        ],
        compiler_params=pltpu.CompilerParams(
            collective_id=0, has_side_effects=True, vmem_limit_bytes=40 << 20
        ),
        name="main",
    )(*[pltpu.with_memory_space_constraint(arg, pltpu.HBM) for arg in args])

    return pl.pallas_call(
        output_kernel,
        out_shape=outs,
        in_specs=[vmem] * 3,
        out_specs=(hbm,) * 3,
        scratch_shapes=[dma((3,))],
        compiler_params=pltpu.CompilerParams(vmem_limit_bytes=4 << 20),
        name="write",
    )(loss, qg, pg)


def solution(mesh):
    return jax.shard_map(
        shards,
        mesh=mesh,
        in_specs=(
            P(("tower", "group", "blk"), None, None),
            P(("tower", "group", "blk"), None),
            P(("tower", "group", "blk"), None),
            P("group", None),
            P(("group", "blk"), None, None),
            P(("group", "blk"), None),
        ),
        out_specs=(
            P(("tower", "group", "blk"), None),
            P(("tower", "group", "blk"), None, None),
            P(("group", "blk"), "tower", None),
        ),
        check_vma=False,
    )
```
